512 devices in a mesh: chan: 32 (over z, core), tm: 16 (over y, x).
Axes of the slice: x: 4, y: 4, z: 16, core: 2. Of those that a mesh axis runs over, the one named last changes fastest.
Arguments:
- samples: bfloat16 [2048, 128, 512], P('chan', 'tm'), may hold values from -6 to 6
- valid: int32 [2048, 128], P('chan', 'tm'), may hold values 0 or 1
- offsets: int32 [8], replicated, may hold values from 0 to 31
Outputs:
- correlations: bfloat16 [16, 8, 2048, 512], P('tm', None, 'chan')
The draws below stay inside these ranges and needn't reach their ends.
All inputs are finite; a program needn't handle non-finite values. No bound on the sum of `valid` on one device may be relied on, other than what follows from the above.
Results may differ from the reference program's by a relative error of at most 0.0045.
Values may be sent and summed in bfloat16 or wider, within the bound.
A program may use at most 64 MiB of HBM per device.

```python
import math
import jax
import jax.numpy as jnp
from jax import lax

CH_DEV = 64
WIN_DEV = 8
SAMPLES = 512
PAIRS = 8
OFFSET_SPAN = 32
BINS = 256
CHANNELS = 2048
WINDOWS = 128
N_TM = 16


def set_ends(values, own_key, smallest, largest):
    shape = values.shape
    index_at = [jax.random.randint(jax.random.fold_in(own_key, axis), (), 0, shape[axis]) for axis in range(len(shape))]
    values = values.at[tuple(index_at)].set(smallest)
    longest = shape.index(max(shape))
    index_at[longest] = (index_at[longest] + 1) % shape[longest]
    return values.at[tuple(index_at)].set(largest)


def shard_levels(key, extent, shards, low, top_value):
    def one(axis_at, parts):
        steps = jax.random.uniform(jax.random.fold_in(jax.random.fold_in(key, 6), axis_at), (parts,), jnp.float32, low / len(shards), top_value / len(shards))
        return jnp.repeat(jnp.exp(steps), extent[axis_at] // parts).reshape((-1,) + (1,) * (len(extent) - axis_at - 1))

    level = one(*shards[0])
    for cut in shards[1:]:
        level = level * one(*cut)
    return level


def centred(stream_key, dims, scale, bound, cuts=(), kind=jnp.bfloat16):
    entries = jax.random.normal(stream_key, dims, jnp.float32) * scale
    if len(cuts) > 0:
        entries = shard_levels(stream_key, dims, cuts, -0.22, 0.18) * entries
    return jnp.clip(entries, min=-bound, max=bound).astype(kind)


def setup_inputs(seed: int = 0) -> dict:
    streams_of = jax.random.split(jax.random.key(seed), 4)
    samples = centred(streams_of[0], (CHANNELS, WINDOWS, SAMPLES), 1.0, 6.0, ((0, 32), (1, 16)))
    valid = set_ends((jax.random.randint(streams_of[1], (CHANNELS, WINDOWS), 0, 8) < 7).astype(jnp.int32), jax.random.fold_in(streams_of[1], 1), 0, 1)
    offsets = set_ends(jax.random.randint(streams_of[2], (PAIRS,), 0, OFFSET_SPAN), jax.random.fold_in(streams_of[2], 1), 0, OFFSET_SPAN - 1).astype(jnp.int32)
    return dict(samples=samples, valid=valid, offsets=offsets)


def forward_table(length):
    bins = length // 2
    rows = jnp.arange(length).astype(jnp.int32)
    freqs = (jnp.arange(bins) + 1).astype(jnp.int32)
    angle = jnp.mod(rows[:, None] * freqs[None, :], length).astype(jnp.float32) * (2.0 * math.pi / length)
    return jnp.concatenate([jnp.cos(angle), -jnp.sin(angle)], axis=1).astype(jnp.bfloat16)

def inverse_table(length):
    bins = length // 2
    freqs = (jnp.arange(bins) + 1).astype(jnp.int32)
    lags = jnp.arange(length).astype(jnp.int32)
    angle = jnp.mod(freqs[:, None] * lags[None, :], length).astype(jnp.float32) * (2.0 * math.pi / length)
    return jnp.concatenate([jnp.cos(angle), -jnp.sin(angle)], axis=0)

def whiten(samples, valid, forward):
    chans, wins, length = samples.shape
    bins = length // 2
    raw = jnp.dot(samples.reshape(chans * wins, length), forward, preferred_element_type=jnp.float32)
    raw = raw.reshape(chans, wins, 2 * bins)
    real_part = raw[..., :bins]
    imag_part = raw[..., bins:]
    power = real_part * real_part + imag_part * imag_part
    level = lax.optimization_barrier(jnp.mean(power, axis=-1, keepdims=True))
    scale = valid[..., None].astype(jnp.float32) * lax.rsqrt(power + 0.01 * level + 1e-06)
    return (real_part * scale, imag_part * scale)

def reference(samples, valid, offsets):
    forward = forward_table(SAMPLES)
    inverse = inverse_table(SAMPLES)
    blocks = CHANNELS // CH_DEV
    white_re, white_im = lax.map(lambda pair: whiten(pair[0], pair[1], forward), (samples.reshape(blocks, CH_DEV, WINDOWS, SAMPLES), valid.reshape(blocks, CH_DEV, WINDOWS)))
    white_re = white_re.reshape(CHANNELS, WINDOWS, BINS)
    white_im = white_im.reshape(CHANNELS, WINDOWS, BINS)
    padding = jnp.zeros((OFFSET_SPAN, WINDOWS, BINS), jnp.float32)
    padded_re = jnp.concatenate([white_re, padding], axis=0)
    padded_im = jnp.concatenate([white_im, padding], axis=0)
    position = jnp.arange(WINDOWS).astype(jnp.int32)
    ends = ((jnp.arange(N_TM) + 1) * WIN_DEV).astype(jnp.int32)
    delay = ends[:, None] - 1 - position[None, :]
    weights = jnp.where(delay >= 0, jnp.power(jnp.float32(0.99), jnp.maximum(delay, 0).astype(jnp.float32)), jnp.float32(0.0))

    def block(index):
        start = (index * CH_DEV).astype(jnp.int32)
        ext_re = lax.dynamic_slice_in_dim(padded_re, start, CH_DEV + OFFSET_SPAN, 0)
        ext_im = lax.dynamic_slice_in_dim(padded_im, start, CH_DEV + OFFSET_SPAN, 0)
        own_re = ext_re[:CH_DEV]
        own_im = ext_im[:CH_DEV]

        def one_pair(offset):
            part_re = lax.dynamic_slice_in_dim(ext_re, offset.astype(jnp.int32), CH_DEV, 0)
            part_im = lax.dynamic_slice_in_dim(ext_im, offset.astype(jnp.int32), CH_DEV, 0)
            cross_re = own_re * part_re + own_im * part_im
            cross_im = own_im * part_re - own_re * part_im
            stack_re = jnp.einsum('gw,cwf->gcf', weights, cross_re, precision=lax.Precision.HIGHEST)
            stack_im = jnp.einsum('gw,cwf->gcf', weights, cross_im, precision=lax.Precision.HIGHEST)
            return (stack_re, stack_im)
        stack_re, stack_im = jax.vmap(one_pair)(offsets)
        joined = jnp.concatenate([stack_re, stack_im], axis=-1).reshape(-1, 2 * BINS)
        corr = jnp.dot(joined, inverse, precision=lax.Precision.HIGHEST, preferred_element_type=jnp.float32)
        corr = corr * BINS ** (-0.5)
        corr = corr.reshape(PAIRS, N_TM, CH_DEV, SAMPLES).astype(jnp.bfloat16)
        return jnp.transpose(corr, (1, 0, 2, 3))
    result = lax.map(block, jnp.arange(blocks).astype(jnp.int32))
    return jnp.transpose(result, (1, 2, 0, 3, 4)).reshape(N_TM, PAIRS, CHANNELS, SAMPLES)
```

```python
import functools
import math

import jax
import jax.numpy as jnp
import numpy as np
from jax import lax
from jax.experimental import pallas as pl
from jax.experimental.pallas import tpu as pltpu
from jax.sharding import PartitionSpec as P

OFFSET_SPAN = 32
DECAY = 0.99
MESH = pl.DeviceIdType.MESH
F32 = jnp.float32
BF16 = jnp.bfloat16


def angles(rows, columns, length):
    turn = np.mod(rows[:, None] * columns[None, :], length).astype(np.float32)
    return turn * np.float32(2.0 * math.pi / length)


def forward_table(length):
    angle = angles(np.arange(length), np.arange(length // 2) + 1, length)
    return np.concatenate([np.cos(angle), -np.sin(angle)], axis=1).astype(BF16)


def inverse_table(length):
    angle = angles(np.arange(length // 2) + 1, np.arange(length), length)
    table = np.concatenate([np.cos(angle), -np.sin(angle)], axis=0)
    table = table * np.float32((length // 2) ** -0.5)
    high = table.astype(BF16)
    low = (table - high.astype(np.float32)).astype(BF16)
    return np.stack([high, low])


def kernel(
    n_chan,
    n_tm,
    x_hbm,
    valid_ref,
    offsets_ref,
    forward_hbm,
    inverse_hbm,
    out_ref,
    x,
    x_edge,
    valid_edge,
    forward,
    inverse,
    raw,
    mask,
    white,
    send,
    recv,
    high,
    low,
    done,
    load_sem,
    edge_send,
    edge_recv,
    send_sem,
    recv_sem,
    back_send,
    back_recv,
):
    chan = lax.axis_index("chan")
    me = lax.axis_index("tm")
    span = OFFSET_SPAN
    wins, chans = valid_ref.shape
    rows, length = x.shape
    bins = length // 2
    lanes = 128
    half = bins // lanes
    part = send.shape[2]

    barrier = pltpu.get_barrier_semaphore()

    @pl.loop(1, n_tm)
    def _(step):
        peer = lax.rem(me + step, n_tm)
        pl.semaphore_signal(barrier, inc=1, device_id={"tm": peer}, device_id_type=MESH)

    @pl.when(chan > 0)
    def _():
        pl.semaphore_signal(barrier, inc=1, device_id={"chan": chan - 1}, device_id_type=MESH)

    @pl.when(chan < n_chan - 1)
    def _():
        pl.semaphore_signal(barrier, inc=1, device_id={"chan": chan + 1}, device_id_type=MESH)

    load_x = pltpu.make_async_copy(x_hbm, x, load_sem.at[0])
    load_f = pltpu.make_async_copy(forward_hbm, forward, load_sem.at[1])
    load_i = pltpu.make_async_copy(inverse_hbm, inverse, load_sem.at[2])
    load_x.start()
    load_f.start()
    load_i.start()

    def whiten(source, valid, base, count):
        mask[pl.ds(base, chans), :] = valid[...].astype(F32).T

        def product(i, carry):
            at = pl.multiple_of(i * 128, 128)
            block = jnp.dot(
                source[pl.ds(at, 128), :], forward[...], preferred_element_type=F32
            )
            for l in range(2 * half):
                raw[l, pl.ds(at, 128), :] = block[:, l * lanes : (l + 1) * lanes]
            return carry

        lax.fori_loop(0, count * wins // 128, product, 0)

        def block(i, carry):
            at = pl.multiple_of(i * 8 * wins, 8 * wins)
            to = pl.multiple_of(base + i * 8, 8)
            usable = mask[pl.ds(to, 8), :]
            for w in range(wins):
                values = [raw[l, pl.ds(at + w, 8, stride=wins), :] for l in range(2 * half)]
                power = [
                    values[b] * values[b] + values[half + b] * values[half + b]
                    for b in range(half)
                ]
                level = jnp.sum(sum(power), axis=1, keepdims=True) * (1.0 / bins)
                floor = 0.01 * level + 1e-06
                factor = usable[:, w : w + 1] * (DECAY ** (0.5 * (wins - 1 - w)))
                for b in range(half):
                    scale = factor * lax.rsqrt(power[b] + floor)
                    white[w, b, pl.ds(to, 8), :] = values[b] * scale
                    white[w, half + b, pl.ds(to, 8), :] = values[half + b] * scale
            return carry

        lax.fori_loop(0, count // 8, block, 0)

    load_x.wait()
    load_f.wait()
    whiten(x, valid_ref, 0, chans)

    neighbours = (chan > 0).astype(jnp.int32) + (chan < n_chan - 1).astype(jnp.int32)
    pl.semaphore_wait(barrier, n_tm - 1 + neighbours)

    def edge_copies():
        before = {"chan": lax.max(chan - 1, 0)}
        return (
            pltpu.make_async_remote_copy(
                src_ref=x.at[pl.ds(0, span * wins), :],
                dst_ref=x_edge,
                send_sem=edge_send.at[0],
                recv_sem=edge_recv.at[0],
                device_id=before,
                device_id_type=MESH,
            ),
            pltpu.make_async_remote_copy(
                src_ref=valid_ref,
                dst_ref=valid_edge,
                send_sem=edge_send.at[1],
                recv_sem=edge_recv.at[1],
                device_id=before,
                device_id_type=MESH,
            ),
        )

    @pl.when(chan > 0)
    def _():
        for copy in edge_copies():
            copy.start()

    def piece(phase, owner):
        offset = offsets_ref[owner // 2]
        first = phase * (chans // 2) + lax.rem(owner, 2) * part
        slot = send.at[phase, owner]
        for b in range(half):
            real, imag = [], []
            for c in range(0, part, 8):
                own = pl.multiple_of(first + c, 8)
                other = own + offset
                total_re = jnp.zeros((8, lanes), F32)
                total_im = jnp.zeros((8, lanes), F32)
                for w in range(wins):
                    own_re = white[w, b, pl.ds(own, 8), :]
                    own_im = white[w, half + b, pl.ds(own, 8), :]
                    other_re = white[w, b, pl.ds(other, 8), :]
                    other_im = white[w, half + b, pl.ds(other, 8), :]
                    total_re = total_re + (own_re * other_re + own_im * other_im)
                    total_im = total_im + (own_im * other_re - own_re * other_im)
                real.append(total_re)
                imag.append(total_im)
            slot[:, b * lanes : (b + 1) * lanes] = jnp.concatenate(real, axis=0).astype(BF16)
            slot[:, bins + b * lanes : bins + (b + 1) * lanes] = jnp.concatenate(
                imag, axis=0
            ).astype(BF16)

    def piece_copy(phase, owner):
        return pltpu.make_async_remote_copy(
            src_ref=send.at[phase, owner],
            dst_ref=recv.at[phase, me],
            send_sem=send_sem.at[phase, owner],
            recv_sem=recv_sem.at[phase, me],
            device_id={"tm": owner},
            device_id_type=MESH,
        )

    def piece_arrival(phase, source):
        return pltpu.make_async_remote_copy(
            src_ref=send.at[phase, source],
            dst_ref=recv.at[phase, source],
            send_sem=send_sem.at[phase, source],
            recv_sem=recv_sem.at[phase, source],
            device_id={"tm": source},
            device_id_type=MESH,
        )

    def spread(phase):
        def one(step, carry):
            piece(phase, lax.rem(me + step, n_tm))

            @pl.when(step > 1)
            def _():
                piece_copy(phase, lax.rem(me + step - 1, n_tm)).start()

            return carry

        lax.fori_loop(1, n_tm + 1, one, 0)

    spread(0)

    @pl.when(chan < n_chan - 1)
    def _():
        for copy in edge_copies():
            copy.wait_recv()
        whiten(x_edge, valid_edge, chans, span)

    @pl.when(chan == n_chan - 1)
    def _():
        for w in range(wins):
            for l in range(2 * half):
                white[w, l, chans : chans + span, :] = jnp.zeros((span, lanes), F32)

    spread(1)

    load_i.wait()
    fade = DECAY**wins

    def home(phase):
        return me // 2, phase * (chans // 2) + lax.rem(me, 2) * part

    def back_copy(phase, group):
        pair, first = home(phase)
        return pltpu.make_async_remote_copy(
            src_ref=done.at[phase, group],
            dst_ref=out_ref.at[pair, pl.ds(first, part), :],
            send_sem=back_send.at[phase, group],
            recv_sem=back_recv.at[phase, me],
            device_id={"tm": group},
            device_id_type=MESH,
        )

    def back_arrival(phase, source):
        first = phase * (chans // 2) + lax.rem(source, 2) * part
        return pltpu.make_async_remote_copy(
            src_ref=done.at[phase, source],
            dst_ref=out_ref.at[source // 2, pl.ds(first, part), :],
            send_sem=back_send.at[phase, source],
            recv_sem=back_recv.at[phase, source],
            device_id={"tm": source},
            device_id_type=MESH,
        )

    def finish(phase):
        def scan(group, total):
            @pl.when(group != me)
            def _():
                piece_arrival(phase, group).wait_recv()
                high[pl.ds(group * part, part), :] = recv[phase, group]

            @pl.when(group == me)
            def _():
                high[pl.ds(group * part, part), :] = send[phase, me]

            local = high[pl.ds(group * part, part), :].astype(F32)
            total = total * fade + local
            top = total.astype(BF16)
            high[pl.ds(group * part, part), :] = top
            low[pl.ds(group * part, part), :] = (total - top.astype(F32)).astype(BF16)
            return total

        lax.fori_loop(0, n_tm, scan, jnp.zeros((part, length), F32))

        groups = 128 // part

        def transform(i, carry):
            at = pl.multiple_of(i * 128, 128)
            top = high[pl.ds(at, 128), :]
            lags = jnp.dot(top, inverse[0], preferred_element_type=F32)
            lags += jnp.dot(low[pl.ds(at, 128), :], inverse[0], preferred_element_type=F32)
            lags += jnp.dot(top, inverse[1], preferred_element_type=F32)
            lags = lags.astype(BF16)
            for j in range(groups):
                done[phase, i * groups + j] = lags[j * part : (j + 1) * part]
            return carry

        lax.fori_loop(0, n_tm * part // 128, transform, 0)

        pair, first = home(phase)
        out_ref[pair, pl.ds(pl.multiple_of(first, part), part), :] = done[phase, me]

        @pl.loop(1, n_tm)
        def _(step):
            back_copy(phase, lax.rem(me + step, n_tm)).start()

    finish(0)
    finish(1)

    for phase in range(2):

        @pl.loop(1, n_tm)
        def _(step):
            peer = lax.rem(me + step, n_tm)
            piece_copy(phase, peer).wait_send()
            back_copy(phase, peer).wait_send()

    @pl.when(chan > 0)
    def _():
        for copy in edge_copies():
            copy.wait_send()

    for phase in range(2):

        @pl.loop(1, n_tm)
        def _(step):
            back_arrival(phase, lax.rem(me + n_tm - step, n_tm)).wait_recv()


def per_device(n_chan, n_tm, samples, valid, offsets):
    chans, wins, length = samples.shape
    pairs = offsets.shape[0]
    bins = length // 2
    part = pairs * chans // 2 // n_tm
    rows = chans * wins
    edge = OFFSET_SPAN * wins
    vmem = pltpu.VMEM
    dma = pltpu.SemaphoreType.DMA
    out = pl.pallas_call(
        functools.partial(kernel, n_chan, n_tm),
        out_shape=jax.ShapeDtypeStruct((pairs, chans, length), BF16),
        in_specs=[
            pl.BlockSpec(memory_space=pl.ANY),
            pl.BlockSpec(memory_space=pltpu.VMEM),
            pl.BlockSpec(memory_space=pltpu.SMEM),
            pl.BlockSpec(memory_space=pl.ANY),
            pl.BlockSpec(memory_space=pl.ANY),
        ],
        out_specs=pl.BlockSpec(memory_space=pltpu.VMEM),
        scratch_shapes=[
            vmem((rows, length), BF16),
            vmem((edge, length), BF16),
            vmem((wins, chans), jnp.int32),
            vmem((length, length), BF16),
            vmem((2, length, length), BF16),
            vmem((2 * bins // 128, rows, 128), F32),
            vmem((2 * chans, wins), F32),
            vmem((wins, 2 * bins // 128, chans + OFFSET_SPAN, 128), F32),
            vmem((2, n_tm, part, length), BF16),
            vmem((2, n_tm, part, length), BF16),
            vmem((n_tm * part, length), BF16),
            vmem((n_tm * part, length), BF16),
            vmem((2, n_tm, part, length), BF16),
            dma((3,)),
            dma((2,)),
            dma((2,)),
            dma((2, n_tm)),
            dma((2, n_tm)),
            dma((2, n_tm)),
            dma((2, n_tm)),
        ],
        compiler_params=pltpu.CompilerParams(collective_id=0, has_side_effects=True),
        name="stacks",
    )(
        samples.reshape(rows, length),
        valid.T,
        offsets,
        jnp.asarray(forward_table(length)),
        jnp.asarray(inverse_table(length)),
    )
    return out[None]


def solution(mesh):
    body = functools.partial(per_device, mesh.shape["chan"], mesh.shape["tm"])
    return jax.shard_map(
        body,
        mesh=mesh,
        in_specs=(P("chan", "tm", None), P("chan", "tm"), P()),
        out_specs=P("tm", None, "chan", None),
        check_vma=False,
    )
```

```python
import functools
import math

import jax
import jax.numpy as jnp
import numpy as np
from jax import lax
from jax.experimental import pallas as pl
from jax.experimental.pallas import tpu as pltpu
from jax.sharding import PartitionSpec as P

OFFSET_SPAN = 32
DECAY = 0.99
MESH = pl.DeviceIdType.MESH
F32 = jnp.float32
BF16 = jnp.bfloat16
WHITEN = 16


def angles(rows, columns, length):
    turn = np.mod(rows[:, None] * columns[None, :], length).astype(np.float32)
    return turn * np.float32(2.0 * math.pi / length)


def forward_table(length):
    angle = angles(np.arange(length), np.arange(length // 2) + 1, length)
    return np.concatenate([np.cos(angle), -np.sin(angle)], axis=1).astype(BF16)


def inverse_table(length):
    angle = angles(np.arange(length // 2) + 1, np.arange(length), length)
    table = np.concatenate([np.cos(angle), -np.sin(angle)], axis=0)
    table = table * np.float32((length // 2) ** -0.5)
    high = table.astype(BF16)
    low = (table - high.astype(np.float32)).astype(BF16)
    return np.stack([high, low])


def kernel(
    n_chan,
    n_tm,
    x_hbm,
    valid_ref,
    offsets_ref,
    forward_hbm,
    inverse_hbm,
    out_ref,
    x,
    x_edge,
    valid_edge,
    forward,
    inverse,
    raw,
    mask,
    white,
    send,
    recv,
    lags,
    done,
    load_sem,
    edge_send,
    edge_recv,
    send_sem,
    recv_sem,
    back_send,
    back_recv,
    home_sem,
):
    chan = lax.axis_index("chan")
    me = lax.axis_index("tm")
    span = OFFSET_SPAN
    wins, chans = valid_ref.shape
    pairs = offsets_ref.shape[0]
    rows, length = x.shape
    bins = length // 2
    lanes = 128
    half = bins // lanes
    part = recv.shape[3]
    last = n_tm - 1
    blocks = chans // 16
    share = n_tm // blocks

    barrier = pltpu.get_barrier_semaphore()
    for step in range(1, n_tm):
        peer = (me + step) & last
        pl.semaphore_signal(barrier, inc=1, device_id={"tm": peer}, device_id_type=MESH)

    @pl.when(chan > 0)
    def _():
        pl.semaphore_signal(barrier, inc=1, device_id={"chan": chan - 1}, device_id_type=MESH)

    @pl.when(chan < n_chan - 1)
    def _():
        pl.semaphore_signal(barrier, inc=1, device_id={"chan": chan + 1}, device_id_type=MESH)

    load_x = pltpu.make_async_copy(x_hbm, x, load_sem.at[0])
    load_f = pltpu.make_async_copy(forward_hbm, forward, load_sem.at[1])
    load_i = pltpu.make_async_copy(inverse_hbm, inverse, load_sem.at[2])
    load_x.start()
    load_f.start()
    load_i.start()

    def product(source):
        block = jnp.dot(source[...], forward[...], preferred_element_type=F32)
        for l in range(2 * half):
            raw[l, : source.shape[0], :] = block[:, l * lanes : (l + 1) * lanes]

    def whiten(valid, base, count, group):
        mask[base : base + chans, :] = valid[...].astype(F32).T

        def block(i, carry):
            at = pl.multiple_of(i * group * wins, group * wins)
            to = pl.multiple_of(base + i * group, 8)
            usable = mask[pl.ds(to, group), :]
            for w in range(wins):
                values = [raw[l, pl.ds(at + w, group, stride=wins), :] for l in range(2 * half)]
                power = [
                    values[b] * values[b] + values[half + b] * values[half + b]
                    for b in range(half)
                ]
                level = jnp.sum(sum(power), axis=1, keepdims=True) * (1.0 / bins)
                floor = 0.01 * level + 1e-06
                factor = usable[:, w : w + 1] * (DECAY ** (0.5 * (wins - 1 - w)))
                for b in range(half):
                    scale = factor * lax.rsqrt(power[b] + floor)
                    white[w, b, pl.ds(to, group), :] = values[b] * scale
                    white[w, half + b, pl.ds(to, group), :] = values[half + b] * scale
            return carry

        lax.fori_loop(0, count // group, block, 0)

    def edge_copies():
        before = {"chan": lax.max(chan - 1, 0)}
        return (
            pltpu.make_async_remote_copy(
                src_ref=x.at[pl.ds(0, span * wins), :],
                dst_ref=x_edge,
                send_sem=edge_send.at[0],
                recv_sem=edge_recv.at[0],
                device_id=before,
                device_id_type=MESH,
            ),
            pltpu.make_async_remote_copy(
                src_ref=valid_ref,
                dst_ref=valid_edge,
                send_sem=edge_send.at[1],
                recv_sem=edge_recv.at[1],
                device_id=before,
                device_id_type=MESH,
            ),
        )

    load_x.wait()
    load_f.wait()
    product(x)

    neighbours = (chan > 0).astype(jnp.int32) + (chan < n_chan - 1).astype(jnp.int32)
    pl.semaphore_wait(barrier, n_tm - 1 + neighbours)

    @pl.when(chan > 0)
    def _():
        for copy in edge_copies():
            copy.start()

    whiten(valid_ref, 0, chans, WHITEN)

    def piece(phase, block):
        own = pl.multiple_of(phase * (chans // 2) + block * 8, 8)
        for b in range(half):
            own_re = [white[w, b, pl.ds(own, 8), :] for w in range(wins)]
            own_im = [white[w, half + b, pl.ds(own, 8), :] for w in range(wins)]
            for q in range(share):
                real, imag = [], []
                for k in range(q * (pairs // share), (q + 1) * (pairs // share)):
                    other = own + offsets_ref[k]
                    total_re = jnp.zeros((8, lanes), F32)
                    total_im = jnp.zeros((8, lanes), F32)
                    for w in range(wins):
                        other_re = white[w, b, pl.ds(other, 8), :]
                        other_im = white[w, half + b, pl.ds(other, 8), :]
                        total_re += own_re[w] * other_re + own_im[w] * other_im
                        total_im += own_im[w] * other_re - own_re[w] * other_im
                    real.append(total_re)
                    imag.append(total_im)
                slot = block * share + q
                send[phase, slot, b] = jnp.concatenate(real, axis=0).astype(BF16)
                send[phase, slot, half + b] = jnp.concatenate(imag, axis=0).astype(BF16)

    def piece_copy(phase, owner, source):
        return pltpu.make_async_remote_copy(
            src_ref=send.at[phase, owner],
            dst_ref=recv.at[phase, source],
            send_sem=send_sem.at[phase, owner],
            recv_sem=recv_sem.at[phase, source],
            device_id={"tm": owner},
            device_id_type=MESH,
        )

    def spread(phase):
        def one(step, carry):
            block = ((me >> 2) + step) & (blocks - 1)
            piece(phase, block)
            for q in range(share):
                owner = block * share + ((me + q) & (share - 1))

                @pl.when(owner != me)
                def _():
                    piece_copy(phase, owner, me).start()

            return carry

        lax.fori_loop(1, blocks + 1, one, 0)

    spread(0)

    @pl.when(chan < n_chan - 1)
    def _():
        for copy in edge_copies():
            copy.wait_recv()
        product(x_edge)
        whiten(valid_edge, chans, span, WHITEN)

    @pl.when(chan == n_chan - 1)
    def _():
        for w in range(wins):
            for l in range(2 * half):
                white[w, l, chans : chans + span, :] = jnp.zeros((span, lanes), F32)

    spread(1)

    load_i.wait()
    fade = DECAY**wins
    per = pairs // share

    def home(phase, owner):
        first = phase * (chans // 2) + (owner >> 2) * 8
        return out_ref.at[pl.ds((owner & (share - 1)) * per, per), pl.ds(first, 8), :]

    def back_copy(phase, group, owner):
        return pltpu.make_async_remote_copy(
            src_ref=done.at[phase, group],
            dst_ref=home(phase, owner),
            send_sem=back_send.at[phase, group],
            recv_sem=back_recv.at[phase, owner],
            device_id={"tm": group},
            device_id_type=MESH,
        )

    def home_copy(phase):
        return pltpu.make_async_copy(done.at[phase, me], home(phase, me), home_sem.at[phase])

    def finish(phase):
        recv[phase, me] = send[phase, me]

        @pl.loop(1, n_tm)
        def _(step):
            source = (me - step) & last
            piece_copy(phase, source, source).wait_recv()

        total = None
        for b in range(0, 2 * half, 2):
            block = jnp.concatenate(
                [recv[phase, :, b + i].reshape(n_tm * part, lanes) for i in range(2)], axis=1
            )
            for t in range(2):
                term = jnp.dot(
                    block,
                    inverse[t, b * lanes : (b + 2) * lanes, :],
                    preferred_element_type=F32,
                )
                total = term if total is None else total + term
        lags[...] = total
        state = jnp.zeros((part, length), F32)
        for group in range(n_tm):
            state = state * fade + lags[group * part : (group + 1) * part, :]
            done[phase, group] = state.astype(BF16).reshape(per, 8, length)

        for step in range(1, n_tm):
            back_copy(phase, (me + step) & last, me).start()
        home_copy(phase).start()

    finish(0)
    finish(1)

    for phase in range(2):

        @pl.loop(1, n_tm)
        def _(step):
            peer = (me + step) & last
            piece_copy(phase, peer, me).wait_send()
            back_copy(phase, peer, me).wait_send()

        home_copy(phase).wait()

    @pl.when(chan > 0)
    def _():
        for copy in edge_copies():
            copy.wait_send()

    for phase in range(2):

        @pl.loop(1, n_tm)
        def _(step):
            source = (me - step) & last
            back_copy(phase, source, source).wait_recv()


def per_device(n_chan, n_tm, samples, valid, offsets):
    chans, wins, length = samples.shape
    pairs = offsets.shape[0]
    bins = length // 2
    part = pairs * chans // 2 // n_tm
    rows = chans * wins
    edge = OFFSET_SPAN * wins
    vmem = pltpu.VMEM
    dma = pltpu.SemaphoreType.DMA
    out = pl.pallas_call(
        functools.partial(kernel, n_chan, n_tm),
        out_shape=jax.ShapeDtypeStruct((pairs, chans, length), BF16),
        in_specs=[
            pl.BlockSpec(memory_space=pl.ANY),
            pl.BlockSpec(memory_space=pltpu.VMEM),
            pl.BlockSpec(memory_space=pltpu.SMEM),
            pl.BlockSpec(memory_space=pl.ANY),
            pl.BlockSpec(memory_space=pl.ANY),
        ],
        out_specs=pl.BlockSpec(memory_space=pl.ANY),
        scratch_shapes=[
            vmem((rows, length), BF16),
            vmem((edge, length), BF16),
            vmem((wins, chans), jnp.int32),
            vmem((length, length), BF16),
            vmem((2, length, length), BF16),
            vmem((2 * bins // 128, rows, 128), F32),
            vmem((2 * chans, wins), F32),
            vmem((wins, 2 * bins // 128, chans + OFFSET_SPAN, 128), F32),
            vmem((2, n_tm, length // 128, part, 128), BF16),
            vmem((2, n_tm, length // 128, part, 128), BF16),
            vmem((n_tm * part, length), F32),
            vmem((2, n_tm, part // 8, 8, length), BF16),
            dma((3,)),
            dma((2,)),
            dma((2,)),
            dma((2, n_tm)),
            dma((2, n_tm)),
            dma((2, n_tm)),
            dma((2, n_tm)),
            dma((2,)),
        ],
        compiler_params=pltpu.CompilerParams(collective_id=0, has_side_effects=True),
        name="stacks",
    )(
        samples.reshape(rows, length),
        valid.T,
        offsets,
        jnp.asarray(forward_table(length)),
        jnp.asarray(inverse_table(length)),
    )
    return out[None]


def solution(mesh):
    body = functools.partial(per_device, mesh.shape["chan"], mesh.shape["tm"])
    return jax.shard_map(
        body,
        mesh=mesh,
        in_specs=(P("chan", "tm", None), P("chan", "tm"), P()),
        out_specs=P("tm", None, "chan", None),
        check_vma=False,
    )
```

```python
import functools
import math

import jax
import jax.numpy as jnp
import numpy as np
from jax import lax
from jax.experimental import pallas as pl
from jax.experimental.pallas import tpu as pltpu
from jax.sharding import PartitionSpec as P

OFFSET_SPAN = 32
DECAY = 0.99
MESH = pl.DeviceIdType.MESH
F32 = jnp.float32
BF16 = jnp.bfloat16
WHITEN = 16
FAR_FIRST = (10, 2, 8, 6, 14, 9, 11, 5, 7, 13, 15, 1, 3, 4, 12)


def angles(rows, columns, length):
    turn = np.mod(rows[:, None] * columns[None, :], length).astype(np.float32)
    return turn * np.float32(2.0 * math.pi / length)


def forward_table(length):
    angle = angles(np.arange(length), np.arange(length // 2) + 1, length)
    return np.concatenate([np.cos(angle), -np.sin(angle)], axis=1).astype(BF16)


def inverse_table(length):
    angle = angles(np.arange(length // 2) + 1, np.arange(length), length)
    table = np.concatenate([np.cos(angle), -np.sin(angle)], axis=0)
    table = table * np.float32((length // 2) ** -0.5)
    high = table.astype(BF16)
    low = (table - high.astype(np.float32)).astype(BF16)
    return np.stack([high, low])


def kernel(
    n_chan,
    n_tm,
    x_hbm,
    valid_hbm,
    offsets_hbm,
    forward_hbm,
    inverse_hbm,
    out_ref,
    valid_ref,
    offsets_ref,
    x,
    x_edge,
    valid_edge,
    forward,
    inverse,
    raw,
    mask,
    white,
    send,
    recv,
    lags,
    done,
    load_sem,
    edge_send,
    edge_recv,
    send_sem,
    recv_sem,
    back_send,
    back_recv,
    home_sem,
):
    chan = lax.axis_index("chan")
    me = lax.axis_index("tm")
    span = OFFSET_SPAN
    wins, chans = valid_ref.shape
    pairs = offsets_ref.shape[0]
    rows, length = x.shape
    bins = length // 2
    lanes = 128
    half = bins // lanes
    part = recv.shape[3]
    last = n_tm - 1
    blocks = chans // 16
    share = n_tm // blocks

    loads = [
        pltpu.make_async_copy(source, target, load_sem.at[i])
        for i, (source, target) in enumerate(
            (
                (x_hbm, x),
                (forward_hbm, forward),
                (valid_hbm, valid_ref),
                (offsets_hbm, offsets_ref),
                (inverse_hbm, inverse),
            )
        )
    ]
    for load in loads:
        load.start()

    barrier = pltpu.get_barrier_semaphore()
    for step in FAR_FIRST:
        peer = (me ^ step) & last
        pl.semaphore_signal(barrier, inc=1, device_id={"tm": peer}, device_id_type=MESH)

    @pl.when(chan > 0)
    def _():
        pl.semaphore_signal(barrier, inc=1, device_id={"chan": chan - 1}, device_id_type=MESH)

    @pl.when(chan < n_chan - 1)
    def _():
        pl.semaphore_signal(barrier, inc=1, device_id={"chan": chan + 1}, device_id_type=MESH)

    def product(source):
        block = jnp.dot(source[...], forward[...], preferred_element_type=F32)
        for l in range(2 * half):
            raw[l, : block.shape[0], :] = block[:, l * lanes : (l + 1) * lanes]

    def whiten(base, count, group):
        def block(i, carry):
            at = pl.multiple_of(i * group * wins, group * wins)
            to = pl.multiple_of(base + i * group, group)
            usable = mask[pl.ds(to, group), :]
            for w in range(wins):
                values = [raw[l, pl.ds(at + w, group, stride=wins), :] for l in range(2 * half)]
                power = [
                    values[b] * values[b] + values[half + b] * values[half + b]
                    for b in range(half)
                ]
                level = jnp.sum(sum(power), axis=1, keepdims=True) * (1.0 / bins)
                floor = 0.01 * level + 1e-06
                factor = usable[:, w : w + 1] * (DECAY ** (0.5 * (wins - 1 - w)))
                for b in range(half):
                    scale = factor * lax.rsqrt(power[b] + floor)
                    white[w, b, pl.ds(to, group), :] = values[b] * scale
                    white[w, half + b, pl.ds(to, group), :] = values[half + b] * scale
            return carry

        lax.fori_loop(0, count // group, block, 0)

    before = {"chan": lax.max(chan - 1, 0)}
    flags = pltpu.make_async_remote_copy(
        src_ref=valid_ref,
        dst_ref=valid_edge,
        send_sem=edge_send.at[span // 8],
        recv_sem=edge_recv.at[span // 8],
        device_id=before,
        device_id_type=MESH,
    )

    def edge_copy(i):
        at = pl.ds(pl.multiple_of(i * 8 * wins, 8 * wins), 8 * wins)
        return pltpu.make_async_remote_copy(
            src_ref=x.at[at, :],
            dst_ref=x_edge.at[at, :],
            send_sem=edge_send.at[i],
            recv_sem=edge_recv.at[i],
            device_id=before,
            device_id_type=MESH,
        )

    loads[0].wait()
    loads[1].wait()
    product(x)
    loads[2].wait()
    loads[3].wait()

    neighbours = (chan > 0).astype(jnp.int32) + (chan < n_chan - 1).astype(jnp.int32)
    pl.semaphore_wait(barrier, n_tm - 1 + neighbours)

    @pl.when(chan > 0)
    def _():
        flags.start()
        for i in range(span // 8):
            edge_copy(i).start()

    mask[:chans, :] = valid_ref[...].astype(F32).T
    whiten(0, chans, WHITEN)

    def owner_of(block, q):
        return q * share + ((block - q) & (share - 1))

    def block_of(owner):
        return ((owner >> 2) + owner) & (share - 1)

    def piece(phase, block):
        own = pl.multiple_of(phase * (chans // 2) + block * 8, 8)
        for b in range(half):
            own_re = [white[w, b, pl.ds(own, 8), :] for w in range(wins)]
            own_im = [white[w, half + b, pl.ds(own, 8), :] for w in range(wins)]
            for q in range(share):
                real, imag = [], []
                for k in range(q * (pairs // share), (q + 1) * (pairs // share)):
                    other = own + offsets_ref[k]
                    total_re = jnp.zeros((8, lanes), F32)
                    total_im = jnp.zeros((8, lanes), F32)
                    for w in range(wins):
                        other_re = white[w, b, pl.ds(other, 8), :]
                        other_im = white[w, half + b, pl.ds(other, 8), :]
                        total_re += own_re[w] * other_re + own_im[w] * other_im
                        total_im += own_im[w] * other_re - own_re[w] * other_im
                    real.append(total_re)
                    imag.append(total_im)
                slot = owner_of(block, q)
                send[phase, slot, b] = jnp.concatenate(real, axis=0).astype(BF16)
                send[phase, slot, half + b] = jnp.concatenate(imag, axis=0).astype(BF16)

    def piece_copy(phase, owner, source):
        return pltpu.make_async_remote_copy(
            src_ref=send.at[phase, owner],
            dst_ref=recv.at[phase, source],
            send_sem=send_sem.at[phase, owner],
            recv_sem=recv_sem.at[phase, source],
            device_id={"tm": owner},
            device_id_type=MESH,
        )

    def deliver(phase, block):
        piece(phase, block)
        for i in range(share):
            owner = owner_of(block, (me + i) & (share - 1))

            @pl.when(owner != me)
            def _():
                piece_copy(phase, owner, me).start()

    def inner(step, carry):
        deliver(0, (block_of(me) + step) & (blocks - 1))
        return carry

    lax.fori_loop(1, blocks + 1, inner, 0)

    @pl.when(chan < n_chan - 1)
    def _():
        flags.wait_recv()
        mask[chans:, :] = valid_edge[...].astype(F32).T

    @pl.when(chan == n_chan - 1)
    def _():
        for w in range(wins):
            for l in range(2 * half):
                white[w, l, chans : chans + span, :] = jnp.zeros((span, lanes), F32)

    def outer(block, carry):
        @pl.when(chan < n_chan - 1)
        def _():
            edge_copy(block).wait_recv()
            product(x_edge.at[pl.ds(pl.multiple_of(block * 8 * wins, 8 * wins), 8 * wins), :])
            whiten(chans + block * 8, 8, 8)

        deliver(1, block)
        return carry

    lax.fori_loop(0, blocks, outer, 0)

    loads[4].wait()
    fade = DECAY**wins
    per = pairs // share

    def home(phase, owner):
        first = phase * (chans // 2) + block_of(owner) * 8
        return out_ref.at[pl.ds((owner >> 2) * per, per), pl.ds(first, 8), :]

    def back_copy(phase, group, owner):
        return pltpu.make_async_remote_copy(
            src_ref=done.at[phase, group],
            dst_ref=home(phase, owner),
            send_sem=back_send.at[phase, group],
            recv_sem=back_recv.at[phase, owner],
            device_id={"tm": group},
            device_id_type=MESH,
        )

    def home_copy(phase):
        return pltpu.make_async_copy(done.at[phase, me], home(phase, me), home_sem.at[phase])

    def finish(phase):
        recv[phase, me] = send[phase, me]

        @pl.loop(1, n_tm)
        def _(step):
            source = (me - step) & last
            piece_copy(phase, source, source).wait_recv()

        total = None
        for b in range(0, 2 * half, 2):
            block = jnp.concatenate(
                [recv[phase, :, b + i].reshape(n_tm * part, lanes) for i in range(2)], axis=1
            )
            for t in range(2):
                term = jnp.dot(
                    block,
                    inverse[t, b * lanes : (b + 2) * lanes, :],
                    preferred_element_type=F32,
                )
                total = term if total is None else total + term
        lags[...] = total
        state = jnp.zeros((part, length), F32)
        for group in range(n_tm):
            state = state * fade + lags[group * part : (group + 1) * part, :]
            done[phase, group] = state.astype(BF16).reshape(per, 8, length)

        for step in range(1, n_tm):
            back_copy(phase, (me + step) & last, me).start()
        home_copy(phase).start()

    finish(0)
    finish(1)

    for phase in range(2):

        @pl.loop(1, n_tm)
        def _(step):
            peer = (me + step) & last
            piece_copy(phase, peer, me).wait_send()
            back_copy(phase, peer, me).wait_send()

        home_copy(phase).wait()

    @pl.when(chan > 0)
    def _():
        flags.wait_send()
        for i in range(span // 8):
            edge_copy(i).wait_send()

    for phase in range(2):

        @pl.loop(1, n_tm)
        def _(step):
            source = (me - step) & last
            back_copy(phase, source, source).wait_recv()


def per_device(n_chan, n_tm, samples, valid, offsets):
    chans, wins, length = samples.shape
    pairs = offsets.shape[0]
    bins = length // 2
    part = pairs * chans // 2 // n_tm
    rows = chans * wins
    edge = OFFSET_SPAN * wins
    vmem = pltpu.VMEM
    dma = pltpu.SemaphoreType.DMA
    out = pl.pallas_call(
        functools.partial(kernel, n_chan, n_tm),
        out_shape=pltpu.VMEM((pairs, chans, length), BF16),
        in_specs=[pl.BlockSpec(memory_space=pltpu.HBM)] * 5,
        out_specs=pl.BlockSpec(memory_space=pl.ANY),
        scratch_shapes=[
            vmem((wins, chans), jnp.int32),
            pltpu.SMEM((pairs,), jnp.int32),
            vmem((rows, length), BF16),
            vmem((edge, length), BF16),
            vmem((wins, chans), jnp.int32),
            vmem((length, length), BF16),
            vmem((2, length, length), BF16),
            vmem((2 * bins // 128, rows, 128), F32),
            vmem((2 * chans, wins), F32),
            vmem((wins, 2 * bins // 128, chans + OFFSET_SPAN, 128), F32),
            vmem((2, n_tm, length // 128, part, 128), BF16),
            vmem((2, n_tm, length // 128, part, 128), BF16),
            vmem((n_tm * part, length), F32),
            vmem((2, n_tm, part // 8, 8, length), BF16),
            dma((5,)),
            dma((OFFSET_SPAN // 8 + 1,)),
            dma((OFFSET_SPAN // 8 + 1,)),
            dma((2, n_tm)),
            dma((2, n_tm)),
            dma((2, n_tm)),
            dma((2, n_tm)),
            dma((2,)),
        ],
        compiler_params=pltpu.CompilerParams(
            collective_id=0, has_side_effects=True
        ),
        name="stacks",
    )(
        samples.reshape(rows, length),
        valid.T,
        offsets,
        jnp.asarray(forward_table(length)),
        jnp.asarray(inverse_table(length)),
    )
    return out[None]


def solution(mesh):
    body = functools.partial(per_device, mesh.shape["chan"], mesh.shape["tm"])
    return jax.shard_map(
        body,
        mesh=mesh,
        in_specs=(P("chan", "tm", None), P("chan", "tm"), P()),
        out_specs=P("tm", None, "chan", None),
        check_vma=False,
    )
```

```python
import functools
import math

import jax
import jax.numpy as jnp
import numpy as np
from jax import lax
from jax.experimental import pallas as pl
from jax.experimental.pallas import tpu as pltpu
from jax.sharding import PartitionSpec as P

OFFSET_SPAN = 32
DECAY = 0.99
MESH = pl.DeviceIdType.MESH
F32 = jnp.float32
BF16 = jnp.bfloat16
WHITEN = 16
FAR_FIRST = (10, 2, 8, 6, 14, 9, 11, 5, 7, 13, 15, 1, 3, 4, 12)


def angles(rows, columns, length):
    turn = np.mod(rows[:, None] * columns[None, :], length).astype(np.float32)
    return turn * np.float32(2.0 * math.pi / length)


def forward_table(length):
    angle = angles(np.arange(length), np.arange(length // 2) + 1, length)
    return np.concatenate([np.cos(angle), -np.sin(angle)], axis=1).astype(BF16)


def inverse_table(length):
    angle = angles(np.arange(length // 2) + 1, np.arange(length), length)
    table = np.concatenate([np.cos(angle), -np.sin(angle)], axis=0)
    table = table * np.float32((length // 2) ** -0.5)
    high = table.astype(BF16)
    low = (table - high.astype(np.float32)).astype(BF16)
    return np.stack([high, low])


def kernel(
    n_chan,
    n_tm,
    x_hbm,
    valid_hbm,
    offsets_hbm,
    forward_hbm,
    inverse_hbm,
    out_ref,
    valid_ref,
    offsets_ref,
    x,
    x_edge,
    valid_edge,
    forward,
    inverse,
    raw,
    mask,
    white,
    send,
    recv,
    lags,
    done,
    load_sem,
    edge_send,
    edge_recv,
    send_sem,
    recv_sem,
    back_send,
    back_recv,
    home_sem,
):
    chan = lax.axis_index("chan")
    me = lax.axis_index("tm")
    span = OFFSET_SPAN
    wins, chans = valid_ref.shape
    pairs = offsets_ref.shape[0]
    rows, length = x.shape
    bins = length // 2
    lanes = 128
    half = bins // lanes
    part = recv.shape[3]
    last = n_tm - 1
    blocks = chans // 16
    share = n_tm // blocks

    loads = [
        pltpu.make_async_copy(source, target, load_sem.at[i])
        for i, (source, target) in enumerate(
            (
                (x_hbm, x),
                (forward_hbm, forward),
                (valid_hbm, valid_ref),
                (offsets_hbm, offsets_ref),
                (inverse_hbm, inverse),
            )
        )
    ]
    for load in loads:
        load.start()

    barrier = pltpu.get_barrier_semaphore()
    for step in FAR_FIRST:
        peer = (me ^ step) & last
        pl.semaphore_signal(barrier, inc=1, device_id={"tm": peer}, device_id_type=MESH)

    @pl.when(chan > 0)
    def _():
        pl.semaphore_signal(barrier, inc=1, device_id={"chan": chan - 1}, device_id_type=MESH)

    @pl.when(chan < n_chan - 1)
    def _():
        pl.semaphore_signal(barrier, inc=1, device_id={"chan": chan + 1}, device_id_type=MESH)

    def product(source):
        block = jnp.dot(source[...], forward[...], preferred_element_type=F32)
        for l in range(2 * half):
            raw[l, : block.shape[0], :] = block[:, l * lanes : (l + 1) * lanes]

    def whiten(base, count, group):
        def block(i, carry):
            at = pl.multiple_of(i * group * wins, group * wins)
            to = pl.multiple_of(base + i * group, group)
            usable = mask[pl.ds(to, group), :]
            for w in range(wins):
                values = [raw[l, pl.ds(at + w, group, stride=wins), :] for l in range(2 * half)]
                power = [
                    values[b] * values[b] + values[half + b] * values[half + b]
                    for b in range(half)
                ]
                level = jnp.sum(sum(power), axis=1, keepdims=True) * (1.0 / bins)
                floor = 0.01 * level + 1e-06
                factor = usable[:, w : w + 1] * (DECAY ** (0.5 * (wins - 1 - w)))
                for b in range(half):
                    scale = factor * lax.rsqrt(power[b] + floor)
                    white[w, b, pl.ds(to, group), :] = values[b] * scale
                    white[w, half + b, pl.ds(to, group), :] = values[half + b] * scale
            return carry

        lax.fori_loop(0, count // group, block, 0)

    before = {"chan": lax.max(chan - 1, 0)}
    flags = pltpu.make_async_remote_copy(
        src_ref=valid_ref,
        dst_ref=valid_edge,
        send_sem=edge_send.at[span // 8],
        recv_sem=edge_recv.at[span // 8],
        device_id=before,
        device_id_type=MESH,
    )

    def edge_copy(i):
        at = pl.ds(pl.multiple_of(i * 8 * wins, 8 * wins), 8 * wins)
        return pltpu.make_async_remote_copy(
            src_ref=x.at[at, :],
            dst_ref=x_edge.at[at, :],
            send_sem=edge_send.at[i],
            recv_sem=edge_recv.at[i],
            device_id=before,
            device_id_type=MESH,
        )

    loads[0].wait()
    loads[1].wait()
    product(x)
    loads[2].wait()
    loads[3].wait()
    mask[:chans, :] = valid_ref[...].astype(F32).T
    whiten(0, chans, WHITEN)

    neighbours = (chan > 0).astype(jnp.int32) + (chan < n_chan - 1).astype(jnp.int32)
    pl.semaphore_wait(barrier, n_tm - 1 + neighbours)

    @pl.when(chan > 0)
    def _():
        flags.start()
        for i in range(span // 8):
            edge_copy(i).start()


    def owner_of(block, q):
        return q * share + block

    def block_of(owner):
        return owner & 3

    def piece(phase, block):
        own = pl.multiple_of(phase * (chans // 2) + block * 8, 8)
        for b in range(half):
            own_re = [white[w, b, pl.ds(own, 8), :] for w in range(wins)]
            own_im = [white[w, half + b, pl.ds(own, 8), :] for w in range(wins)]
            for q in range(share):
                real, imag = [], []
                for k in range(q * (pairs // share), (q + 1) * (pairs // share)):
                    other = own + offsets_ref[k]
                    total_re = jnp.zeros((8, lanes), F32)
                    total_im = jnp.zeros((8, lanes), F32)
                    for w in range(wins):
                        other_re = white[w, b, pl.ds(other, 8), :]
                        other_im = white[w, half + b, pl.ds(other, 8), :]
                        total_re += own_re[w] * other_re + own_im[w] * other_im
                        total_im += own_im[w] * other_re - own_re[w] * other_im
                    real.append(total_re)
                    imag.append(total_im)
                slot = owner_of(block, q)
                send[phase, slot, b] = jnp.concatenate(real, axis=0).astype(BF16)
                send[phase, slot, half + b] = jnp.concatenate(imag, axis=0).astype(BF16)

    def piece_copy(phase, owner, source):
        return pltpu.make_async_remote_copy(
            src_ref=send.at[phase, owner],
            dst_ref=recv.at[phase, source],
            send_sem=send_sem.at[phase, owner],
            recv_sem=recv_sem.at[phase, source],
            device_id={"tm": owner},
            device_id_type=MESH,
        )

    def deliver(phase, block):
        piece(phase, block)
        for i in range(share):
            owner = owner_of(block, (me + i) & (share - 1))

            @pl.when(owner != me)
            def _():
                piece_copy(phase, owner, me).start()

    def inner(step, carry):
        deliver(0, (block_of(me) + step) & (blocks - 1))
        return carry

    lax.fori_loop(1, blocks + 1, inner, 0)

    @pl.when(chan < n_chan - 1)
    def _():
        flags.wait_recv()
        mask[chans:, :] = valid_edge[...].astype(F32).T

    @pl.when(chan == n_chan - 1)
    def _():
        for w in range(wins):
            for l in range(2 * half):
                white[w, l, chans : chans + span, :] = jnp.zeros((span, lanes), F32)

    def outer(block, carry):
        @pl.when(chan < n_chan - 1)
        def _():
            edge_copy(block).wait_recv()
            product(x_edge.at[pl.ds(pl.multiple_of(block * 8 * wins, 8 * wins), 8 * wins), :])
            whiten(chans + block * 8, 8, 8)

        deliver(1, block)
        return carry

    lax.fori_loop(0, blocks, outer, 0)

    loads[4].wait()
    fade = DECAY**wins
    per = pairs // share

    def home(phase, owner):
        first = phase * (chans // 2) + block_of(owner) * 8
        return out_ref.at[pl.ds((owner >> 2) * per, per), pl.ds(first, 8), :]

    def back_copy(phase, group, owner):
        return pltpu.make_async_remote_copy(
            src_ref=done.at[phase, group],
            dst_ref=home(phase, owner),
            send_sem=back_send.at[phase, group],
            recv_sem=back_recv.at[phase, owner],
            device_id={"tm": group},
            device_id_type=MESH,
        )

    def home_copy(phase):
        return pltpu.make_async_copy(done.at[phase, me], home(phase, me), home_sem.at[phase])

    def finish(phase):
        recv[phase, me] = send[phase, me]

        @pl.loop(1, n_tm)
        def _(step):
            source = (me - step) & last
            piece_copy(phase, source, source).wait_recv()

        total = None
        for b in range(0, 2 * half, 2):
            block = jnp.concatenate(
                [recv[phase, :, b + i].reshape(n_tm * part, lanes) for i in range(2)], axis=1
            )
            for t in range(2):
                term = jnp.dot(
                    block,
                    inverse[t, b * lanes : (b + 2) * lanes, :],
                    preferred_element_type=F32,
                )
                total = term if total is None else total + term
        lags[...] = total
        state = jnp.zeros((part, length), F32)
        for group in range(n_tm):
            state = state * fade + lags[group * part : (group + 1) * part, :]
            done[phase, group] = state.astype(BF16).reshape(per, 8, length)

        for step in range(1, n_tm):
            back_copy(phase, (me + step) & last, me).start()
        home_copy(phase).start()

    finish(0)
    finish(1)

    for phase in range(2):

        @pl.loop(1, n_tm)
        def _(step):
            peer = (me + step) & last
            piece_copy(phase, peer, me).wait_send()
            back_copy(phase, peer, me).wait_send()

        home_copy(phase).wait()

    @pl.when(chan > 0)
    def _():
        flags.wait_send()
        for i in range(span // 8):
            edge_copy(i).wait_send()

    for phase in range(2):

        @pl.loop(1, n_tm)
        def _(step):
            source = (me - step) & last
            back_copy(phase, source, source).wait_recv()


def per_device(n_chan, n_tm, samples, valid, offsets):
    chans, wins, length = samples.shape
    pairs = offsets.shape[0]
    bins = length // 2
    part = pairs * chans // 2 // n_tm
    rows = chans * wins
    edge = OFFSET_SPAN * wins
    vmem = pltpu.VMEM
    dma = pltpu.SemaphoreType.DMA
    out = pl.pallas_call(
        functools.partial(kernel, n_chan, n_tm),
        out_shape=pltpu.VMEM((pairs, chans, length), BF16),
        in_specs=[pl.BlockSpec(memory_space=pltpu.HBM)] * 5,
        out_specs=pl.BlockSpec(memory_space=pl.ANY),
        scratch_shapes=[
            vmem((wins, chans), jnp.int32),
            pltpu.SMEM((pairs,), jnp.int32),
            vmem((rows, length), BF16),
            vmem((edge, length), BF16),
            vmem((wins, chans), jnp.int32),
            vmem((length, length), BF16),
            vmem((2, length, length), BF16),
            vmem((2 * bins // 128, rows, 128), F32),
            vmem((2 * chans, wins), F32),
            vmem((wins, 2 * bins // 128, chans + OFFSET_SPAN, 128), F32),
            vmem((2, n_tm, length // 128, part, 128), BF16),
            vmem((2, n_tm, length // 128, part, 128), BF16),
            vmem((n_tm * part, length), F32),
            vmem((2, n_tm, part // 8, 8, length), BF16),
            dma((5,)),
            dma((OFFSET_SPAN // 8 + 1,)),
            dma((OFFSET_SPAN // 8 + 1,)),
            dma((2, n_tm)),
            dma((2, n_tm)),
            dma((2, n_tm)),
            dma((2, n_tm)),
            dma((2,)),
        ],
        compiler_params=pltpu.CompilerParams(
            collective_id=0, has_side_effects=True
        ),
        name="stacks",
    )(
        samples.reshape(rows, length),
        valid.T,
        offsets,
        jnp.asarray(forward_table(length)),
        jnp.asarray(inverse_table(length)),
    )
    return out[None]


def solution(mesh):
    body = functools.partial(per_device, mesh.shape["chan"], mesh.shape["tm"])
    return jax.shard_map(
        body,
        mesh=mesh,
        in_specs=(P("chan", "tm", None), P("chan", "tm"), P()),
        out_specs=P("tm", None, "chan", None),
        check_vma=False,
    )
```

```python
import functools
import math

import jax
import jax.numpy as jnp
import numpy as np
from jax import lax
from jax.experimental import pallas as pl
from jax.experimental.pallas import tpu as pltpu
from jax.sharding import PartitionSpec as P

OFFSET_SPAN = 32
DECAY = 0.99
MESH = pl.DeviceIdType.MESH
F32 = jnp.float32
BF16 = jnp.bfloat16
WHITEN = 16
FAR_FIRST = (10, 2, 8, 6, 14, 9, 11, 5, 7, 13, 15, 1, 3, 4, 12)


def angles(rows, columns, length):
    turn = np.mod(rows[:, None] * columns[None, :], length).astype(np.float32)
    return turn * np.float32(2.0 * math.pi / length)


def forward_table(length):
    angle = angles(np.arange(length), np.arange(length // 2) + 1, length)
    return np.concatenate([np.cos(angle), -np.sin(angle)], axis=1).astype(BF16)


def inverse_table(length):
    angle = angles(np.arange(length // 2) + 1, np.arange(length), length)
    table = np.concatenate([np.cos(angle), -np.sin(angle)], axis=0)
    table = table * np.float32((length // 2) ** -0.5)
    high = table.astype(BF16)
    low = (table - high.astype(np.float32)).astype(BF16)
    return np.stack([high, low])


def kernel(
    n_chan,
    n_tm,
    x_hbm,
    valid_hbm,
    offsets_hbm,
    forward_hbm,
    inverse_hbm,
    out_ref,
    valid_ref,
    offsets_ref,
    x,
    x_edge,
    valid_edge,
    forward,
    inverse,
    raw,
    mask,
    white,
    send,
    recv,
    lags,
    done,
    load_sem,
    edge_send,
    edge_recv,
    send_sem,
    recv_sem,
    back_send,
    back_recv,
    home_sem,
):
    chan = lax.axis_index("chan")
    me = lax.axis_index("tm")
    span = OFFSET_SPAN
    wins, chans = valid_ref.shape
    pairs = offsets_ref.shape[0]
    rows, length = x.shape
    bins = length // 2
    lanes = 128
    half = bins // lanes
    part = recv.shape[3]
    last = n_tm - 1
    blocks = chans // 16
    share = n_tm // blocks

    loads = [
        pltpu.make_async_copy(source, target, load_sem.at[i])
        for i, (source, target) in enumerate(
            (
                (x_hbm, x),
                (forward_hbm, forward),
                (valid_hbm, valid_ref),
                (offsets_hbm, offsets_ref),
                (inverse_hbm, inverse),
            )
        )
    ]
    for load in loads:
        load.start()

    barrier = pltpu.get_barrier_semaphore()
    for step in FAR_FIRST:
        peer = (me ^ step) & last
        pl.semaphore_signal(barrier, inc=1, device_id={"tm": peer}, device_id_type=MESH)

    @pl.when(chan > 0)
    def _():
        pl.semaphore_signal(barrier, inc=1, device_id={"chan": chan - 1}, device_id_type=MESH)

    @pl.when(chan < n_chan - 1)
    def _():
        pl.semaphore_signal(barrier, inc=1, device_id={"chan": chan + 1}, device_id_type=MESH)

    def product(source):
        block = jnp.dot(source[...], forward[...], preferred_element_type=F32)
        for l in range(2 * half):
            raw[l, : block.shape[0], :] = block[:, l * lanes : (l + 1) * lanes]

    def whiten(base, count, group):
        def block(i, carry):
            at = pl.multiple_of(i * group * wins, group * wins)
            to = pl.multiple_of(base + i * group, group)
            usable = mask[pl.ds(to, group), :]
            for w in range(wins):
                values = [raw[l, pl.ds(at + w, group, stride=wins), :] for l in range(2 * half)]
                power = [
                    values[b] * values[b] + values[half + b] * values[half + b]
                    for b in range(half)
                ]
                level = jnp.sum(sum(power), axis=1, keepdims=True) * (1.0 / bins)
                floor = 0.01 * level + 1e-06
                factor = usable[:, w : w + 1] * (DECAY ** (0.5 * (wins - 1 - w)))
                for b in range(half):
                    scale = factor * lax.rsqrt(power[b] + floor)
                    white[w, b, pl.ds(to, group), :] = values[b] * scale
                    white[w, half + b, pl.ds(to, group), :] = values[half + b] * scale
            return carry

        lax.fori_loop(0, count // group, block, 0)

    before = {"chan": lax.max(chan - 1, 0)}
    flags = pltpu.make_async_remote_copy(
        src_ref=valid_ref,
        dst_ref=valid_edge,
        send_sem=edge_send.at[span // 8],
        recv_sem=edge_recv.at[span // 8],
        device_id=before,
        device_id_type=MESH,
    )

    def edge_copy(i):
        at = pl.ds(pl.multiple_of(i * 8 * wins, 8 * wins), 8 * wins)
        return pltpu.make_async_remote_copy(
            src_ref=x.at[at, :],
            dst_ref=x_edge.at[at, :],
            send_sem=edge_send.at[i],
            recv_sem=edge_recv.at[i],
            device_id=before,
            device_id_type=MESH,
        )

    loads[0].wait()
    loads[1].wait()
    product(x)
    loads[2].wait()
    loads[3].wait()
    mask[:chans, :] = valid_ref[...].astype(F32).T
    whiten(0, chans, WHITEN)

    neighbours = (chan > 0).astype(jnp.int32) + (chan < n_chan - 1).astype(jnp.int32)
    pl.semaphore_wait(barrier, n_tm - 1 + neighbours)

    @pl.when(chan > 0)
    def _():
        flags.start()
        for i in range(span // 8):
            edge_copy(i).start()


    def owner_of(block, q):
        return q * share + block

    def block_of(owner):
        return owner & 3

    def piece(phase, block):
        own = pl.multiple_of(phase * (chans // 2) + block * 8, 8)
        for b in range(half):
            own_re = [white[w, b, pl.ds(own, 8), :] for w in range(wins)]
            own_im = [white[w, half + b, pl.ds(own, 8), :] for w in range(wins)]
            for q in range(share):
                real, imag = [], []
                for k in range(q * (pairs // share), (q + 1) * (pairs // share)):
                    other = own + offsets_ref[k]
                    total_re = jnp.zeros((8, lanes), F32)
                    total_im = jnp.zeros((8, lanes), F32)
                    for w in range(wins):
                        other_re = white[w, b, pl.ds(other, 8), :]
                        other_im = white[w, half + b, pl.ds(other, 8), :]
                        total_re += own_re[w] * other_re + own_im[w] * other_im
                        total_im += own_im[w] * other_re - own_re[w] * other_im
                    real.append(total_re)
                    imag.append(total_im)
                slot = owner_of(block, q)
                send[phase, slot, b] = jnp.concatenate(real, axis=0).astype(BF16)
                send[phase, slot, half + b] = jnp.concatenate(imag, axis=0).astype(BF16)

    def piece_copy(phase, owner, source):
        return pltpu.make_async_remote_copy(
            src_ref=send.at[phase, owner],
            dst_ref=recv.at[phase, source],
            send_sem=send_sem.at[phase, owner],
            recv_sem=recv_sem.at[phase, source],
            device_id={"tm": owner},
            device_id_type=MESH,
        )

    def deliver(phase, block):
        piece(phase, block)
        for i in range(share):
            owner = owner_of(block, (me + i) & (share - 1))

            @pl.when(owner != me)
            def _():
                piece_copy(phase, owner, me).start()

    def inner(step, carry):
        deliver(0, (block_of(me) + step) & (blocks - 1))
        return carry

    lax.fori_loop(1, blocks + 1, inner, 0)

    @pl.when(chan < n_chan - 1)
    def _():
        flags.wait_recv()
        mask[chans:, :] = valid_edge[...].astype(F32).T

    @pl.when(chan == n_chan - 1)
    def _():
        for w in range(wins):
            for l in range(2 * half):
                white[w, l, chans : chans + span, :] = jnp.zeros((span, lanes), F32)

    def outer(block, carry):
        @pl.when(chan < n_chan - 1)
        def _():
            edge_copy(block).wait_recv()
            product(x_edge.at[pl.ds(pl.multiple_of(block * 8 * wins, 8 * wins), 8 * wins), :])
            whiten(chans + block * 8, 8, 8)

        deliver(1, block)
        return carry

    lax.fori_loop(0, blocks, outer, 0)

    loads[4].wait()
    fade = DECAY**wins
    per = pairs // share

    def home(phase, owner):
        first = phase * (chans // 2) + block_of(owner) * 8
        return out_ref.at[pl.ds((owner >> 2) * per, per), pl.ds(first, 8), :]

    def back_copy(phase, group, owner):
        return pltpu.make_async_remote_copy(
            src_ref=done.at[phase, group],
            dst_ref=home(phase, owner),
            send_sem=back_send.at[phase, group],
            recv_sem=back_recv.at[phase, owner],
            device_id={"tm": group},
            device_id_type=MESH,
        )

    def home_copy(phase):
        return pltpu.make_async_copy(done.at[phase, me], home(phase, me), home_sem.at[phase])

    def finish(phase):
        recv[phase, me] = send[phase, me]

        @pl.loop(1, n_tm)
        def _(step):
            source = (me - step) & last
            piece_copy(phase, source, source).wait_recv()

        total = None
        for b in range(0, 2 * half, 2):
            block = jnp.concatenate(
                [recv[phase, :, b + i].reshape(n_tm * part, lanes) for i in range(2)], axis=1
            )
            for t in range(2):
                term = jnp.dot(
                    block,
                    inverse[t, b * lanes : (b + 2) * lanes, :],
                    preferred_element_type=F32,
                )
                total = term if total is None else total + term
        lags[...] = total
        state = jnp.zeros((part, length), F32)
        for group in range(n_tm):
            state = state * fade + lags[group * part : (group + 1) * part, :]
            done[phase, group] = state.astype(BF16).reshape(per, 8, length)


    def give(phase):
        for step in range(1, n_tm):
            back_copy(phase, (me + step) & last, me).start()
        home_copy(phase).start()

    early = (chan & 1) == 1
    finish(0)

    @pl.when(early)
    def _():
        give(0)

    finish(1)

    @pl.when(jnp.logical_not(early))
    def _():
        give(0)

    give(1)


    for phase in range(2):

        @pl.loop(1, n_tm)
        def _(step):
            peer = (me + step) & last
            piece_copy(phase, peer, me).wait_send()
            back_copy(phase, peer, me).wait_send()

        home_copy(phase).wait()

    @pl.when(chan > 0)
    def _():
        flags.wait_send()
        for i in range(span // 8):
            edge_copy(i).wait_send()

    for phase in range(2):

        @pl.loop(1, n_tm)
        def _(step):
            source = (me - step) & last
            back_copy(phase, source, source).wait_recv()


def per_device(n_chan, n_tm, samples, valid, offsets):
    chans, wins, length = samples.shape
    pairs = offsets.shape[0]
    bins = length // 2
    part = pairs * chans // 2 // n_tm
    rows = chans * wins
    edge = OFFSET_SPAN * wins
    vmem = pltpu.VMEM
    dma = pltpu.SemaphoreType.DMA
    out = pl.pallas_call(
        functools.partial(kernel, n_chan, n_tm),
        out_shape=pltpu.VMEM((pairs, chans, length), BF16),
        in_specs=[pl.BlockSpec(memory_space=pltpu.HBM)] * 5,
        out_specs=pl.BlockSpec(memory_space=pl.ANY),
        scratch_shapes=[
            vmem((wins, chans), jnp.int32),
            pltpu.SMEM((pairs,), jnp.int32),
            vmem((rows, length), BF16),
            vmem((edge, length), BF16),
            vmem((wins, chans), jnp.int32),
            vmem((length, length), BF16),
            vmem((2, length, length), BF16),
            vmem((2 * bins // 128, rows, 128), F32),
            vmem((2 * chans, wins), F32),
            vmem((wins, 2 * bins // 128, chans + OFFSET_SPAN, 128), F32),
            vmem((2, n_tm, length // 128, part, 128), BF16),
            vmem((2, n_tm, length // 128, part, 128), BF16),
            vmem((n_tm * part, length), F32),
            vmem((2, n_tm, part // 8, 8, length), BF16),
            dma((5,)),
            dma((OFFSET_SPAN // 8 + 1,)),
            dma((OFFSET_SPAN // 8 + 1,)),
            dma((2, n_tm)),
            dma((2, n_tm)),
            dma((2, n_tm)),
            dma((2, n_tm)),
            dma((2,)),
        ],
        compiler_params=pltpu.CompilerParams(
            collective_id=0, has_side_effects=True
        ),
        name="stacks",
    )(
        samples.reshape(rows, length),
        valid.T,
        offsets,
        jnp.asarray(forward_table(length)),
        jnp.asarray(inverse_table(length)),
    )
    return out[None]


def solution(mesh):
    body = functools.partial(per_device, mesh.shape["chan"], mesh.shape["tm"])
    return jax.shard_map(
        body,
        mesh=mesh,
        in_specs=(P("chan", "tm", None), P("chan", "tm"), P()),
        out_specs=P("tm", None, "chan", None),
        check_vma=False,
    )
```

```python
import functools
import math

import jax
import jax.numpy as jnp
import numpy as np
from jax import lax
from jax.experimental import pallas as pl
from jax.experimental.pallas import tpu as pltpu
from jax.sharding import PartitionSpec as P

OFFSET_SPAN = 32
DECAY = 0.99
MESH = pl.DeviceIdType.MESH
F32 = jnp.float32
BF16 = jnp.bfloat16
WHITEN = 16
FAR_FIRST = (10, 2, 8, 6, 14, 9, 11, 5, 7, 13, 15, 1, 3, 4, 12)


def angles(rows, columns, length):
    turn = np.mod(rows[:, None] * columns[None, :], length).astype(np.float32)
    return turn * np.float32(2.0 * math.pi / length)


def forward_table(length):
    angle = angles(np.arange(length), np.arange(length // 2) + 1, length)
    return np.concatenate([np.cos(angle), -np.sin(angle)], axis=1).astype(BF16)


def inverse_table(length):
    angle = angles(np.arange(length // 2) + 1, np.arange(length), length)
    table = np.concatenate([np.cos(angle), -np.sin(angle)], axis=0)
    table = table * np.float32((length // 2) ** -0.5)
    high = table.astype(BF16)
    low = (table - high.astype(np.float32)).astype(BF16)
    return np.stack([high, low])


def kernel(
    n_chan,
    n_tm,
    x_hbm,
    valid_hbm,
    offsets_hbm,
    forward_hbm,
    inverse_hbm,
    out_ref,
    valid_ref,
    offsets_ref,
    x,
    x_edge,
    valid_edge,
    forward,
    inverse,
    raw,
    mask,
    white,
    send,
    recv,
    lags,
    done,
    load_sem,
    edge_send,
    edge_recv,
    send_sem,
    recv_sem,
    back_send,
    back_recv,
    home_sem,
):
    chan = lax.axis_index("chan")
    me = lax.axis_index("tm")
    span = OFFSET_SPAN
    wins, chans = valid_ref.shape
    pairs = offsets_ref.shape[0]
    rows, length = x.shape
    bins = length // 2
    lanes = 128
    half = bins // lanes
    part = recv.shape[3]
    last = n_tm - 1
    blocks = chans // 16
    share = n_tm // blocks

    loads = [
        pltpu.make_async_copy(source, target, load_sem.at[i])
        for i, (source, target) in enumerate(
            (
                (x_hbm, x),
                (forward_hbm, forward),
                (valid_hbm, valid_ref),
                (offsets_hbm, offsets_ref),
                (inverse_hbm, inverse),
            )
        )
    ]
    for load in loads:
        load.start()

    barrier = pltpu.get_barrier_semaphore()
    for step in FAR_FIRST:
        peer = (me ^ step) & last
        pl.semaphore_signal(barrier, inc=1, device_id={"tm": peer}, device_id_type=MESH)

    @pl.when(chan > 0)
    def _():
        pl.semaphore_signal(barrier, inc=1, device_id={"chan": chan - 1}, device_id_type=MESH)

    @pl.when(chan < n_chan - 1)
    def _():
        pl.semaphore_signal(barrier, inc=1, device_id={"chan": chan + 1}, device_id_type=MESH)

    def product(source):
        block = jnp.dot(source[...], forward[...], preferred_element_type=F32)
        for l in range(2 * half):
            raw[l, : block.shape[0], :] = block[:, l * lanes : (l + 1) * lanes]

    def whiten(base, count, group):
        def block(i, carry):
            at = pl.multiple_of(i * group * wins, group * wins)
            to = pl.multiple_of(base + i * group, group)
            usable = mask[pl.ds(to, group), :]
            for w in range(wins):
                values = [raw[l, pl.ds(at + w, group, stride=wins), :] for l in range(2 * half)]
                power = [
                    values[b] * values[b] + values[half + b] * values[half + b]
                    for b in range(half)
                ]
                level = jnp.sum(sum(power), axis=1, keepdims=True) * (1.0 / bins)
                floor = 0.01 * level + 1e-06
                factor = usable[:, w : w + 1] * (DECAY ** (0.5 * (wins - 1 - w)))
                for b in range(half):
                    scale = factor * lax.rsqrt(power[b] + floor)
                    white[w, b, pl.ds(to, group), :] = values[b] * scale
                    white[w, half + b, pl.ds(to, group), :] = values[half + b] * scale
            return carry

        lax.fori_loop(0, count // group, block, 0)

    before = {"chan": lax.max(chan - 1, 0)}
    flags = pltpu.make_async_remote_copy(
        src_ref=valid_ref,
        dst_ref=valid_edge,
        send_sem=edge_send.at[span // 8],
        recv_sem=edge_recv.at[span // 8],
        device_id=before,
        device_id_type=MESH,
    )

    def edge_copy(i):
        at = pl.ds(pl.multiple_of(i * 8 * wins, 8 * wins), 8 * wins)
        return pltpu.make_async_remote_copy(
            src_ref=x.at[at, :],
            dst_ref=x_edge.at[at, :],
            send_sem=edge_send.at[i],
            recv_sem=edge_recv.at[i],
            device_id=before,
            device_id_type=MESH,
        )

    loads[0].wait()
    loads[1].wait()
    product(x)
    loads[2].wait()
    loads[3].wait()
    mask[:chans, :] = valid_ref[...].astype(F32).T
    whiten(0, chans, WHITEN)

    neighbours = (chan > 0).astype(jnp.int32) + (chan < n_chan - 1).astype(jnp.int32)
    pl.semaphore_wait(barrier, n_tm - 1 + neighbours)

    @pl.when(chan > 0)
    def _():
        flags.start()
        for i in range(span // 8):
            edge_copy(i).start()


    def owner_of(block, q):
        return q * share + block

    def block_of(owner):
        return owner & 3

    def piece(phase, block):
        own = pl.multiple_of(phase * (chans // 2) + block * 8, 8)
        for b in range(half):
            own_re = [white[w, b, pl.ds(own, 8), :] for w in range(wins)]
            own_im = [white[w, half + b, pl.ds(own, 8), :] for w in range(wins)]
            for q in range(share):
                real, imag = [], []
                for k in range(q * (pairs // share), (q + 1) * (pairs // share)):
                    other = own + offsets_ref[k]
                    total_re = jnp.zeros((8, lanes), F32)
                    total_im = jnp.zeros((8, lanes), F32)
                    for w in range(wins):
                        other_re = white[w, b, pl.ds(other, 8), :]
                        other_im = white[w, half + b, pl.ds(other, 8), :]
                        total_re += own_re[w] * other_re + own_im[w] * other_im
                        total_im += own_im[w] * other_re - own_re[w] * other_im
                    real.append(total_re)
                    imag.append(total_im)
                slot = owner_of(block, q)
                send[phase, slot, b] = jnp.concatenate(real, axis=0).astype(BF16)
                send[phase, slot, half + b] = jnp.concatenate(imag, axis=0).astype(BF16)

    def piece_copy(phase, owner, source):
        return pltpu.make_async_remote_copy(
            src_ref=send.at[phase, owner],
            dst_ref=recv.at[phase, source],
            send_sem=send_sem.at[phase, owner],
            recv_sem=recv_sem.at[phase, source],
            device_id={"tm": owner},
            device_id_type=MESH,
        )

    def deliver(phase, block):
        piece(phase, block)
        for i in range(share):
            owner = owner_of(block, (me + i) & (share - 1))

            @pl.when(owner != me)
            def _():
                piece_copy(phase, owner, me).start()

    def inner(step, carry):
        deliver(0, (block_of(me) + step) & (blocks - 1))
        return carry

    lax.fori_loop(1, blocks + 1, inner, 0)

    @pl.when(chan < n_chan - 1)
    def _():
        flags.wait_recv()
        mask[chans:, :] = valid_edge[...].astype(F32).T

    @pl.when(chan == n_chan - 1)
    def _():
        for w in range(wins):
            for l in range(2 * half):
                white[w, l, chans : chans + span, :] = jnp.zeros((span, lanes), F32)

    def outer(block, carry):
        @pl.when(chan < n_chan - 1)
        def _():
            edge_copy(block).wait_recv()
            product(x_edge.at[pl.ds(pl.multiple_of(block * 8 * wins, 8 * wins), 8 * wins), :])
            whiten(chans + block * 8, 8, 8)

        deliver(1, block)
        return carry

    lax.fori_loop(0, blocks, outer, 0)

    loads[4].wait()
    fade = DECAY**wins
    per = pairs // share

    def home(phase, owner):
        first = phase * (chans // 2) + block_of(owner) * 8
        return out_ref.at[pl.ds((owner >> 2) * per, per), pl.ds(first, 8), :]

    def back_copy(phase, group, owner):
        return pltpu.make_async_remote_copy(
            src_ref=done.at[phase, group],
            dst_ref=home(phase, owner),
            send_sem=back_send.at[phase, group],
            recv_sem=back_recv.at[phase, owner],
            device_id={"tm": group},
            device_id_type=MESH,
        )

    def home_copy(phase):
        return pltpu.make_async_copy(done.at[phase, me], home(phase, me), home_sem.at[phase])

    def finish(phase):
        recv[phase, me] = send[phase, me]

        @pl.loop(1, n_tm)
        def _(step):
            source = (me - step) & last
            piece_copy(phase, source, source).wait_recv()

        total = None
        for b in range(0, 2 * half, 2):
            block = jnp.concatenate(
                [recv[phase, :, b + i].reshape(n_tm * part, lanes) for i in range(2)], axis=1
            )
            for t in range(2):
                term = jnp.dot(
                    block,
                    inverse[t, b * lanes : (b + 2) * lanes, :],
                    preferred_element_type=F32,
                )
                total = term if total is None else total + term
        lags[...] = total
        state = jnp.zeros((part, length), F32)
        for group in range(n_tm):
            state = state * fade + lags[group * part : (group + 1) * part, :]
            done[phase, group] = state.astype(BF16).reshape(per, 8, length)


    def give(phase):
        for step in range(1, n_tm):
            back_copy(phase, (me + step) & last, me).start()
        home_copy(phase).start()

    early = jnp.logical_or((chan & 1) == 1, chan == 0)
    finish(0)

    @pl.when(early)
    def _():
        give(0)

    finish(1)

    @pl.when(jnp.logical_not(early))
    def _():
        give(0)

    give(1)


    for phase in range(2):

        @pl.loop(1, n_tm)
        def _(step):
            peer = (me + step) & last
            piece_copy(phase, peer, me).wait_send()
            back_copy(phase, peer, me).wait_send()

        home_copy(phase).wait()

    @pl.when(chan > 0)
    def _():
        flags.wait_send()
        for i in range(span // 8):
            edge_copy(i).wait_send()

    for phase in range(2):

        @pl.loop(1, n_tm)
        def _(step):
            source = (me - step) & last
            back_copy(phase, source, source).wait_recv()


def per_device(n_chan, n_tm, samples, valid, offsets):
    chans, wins, length = samples.shape
    pairs = offsets.shape[0]
    bins = length // 2
    part = pairs * chans // 2 // n_tm
    rows = chans * wins
    edge = OFFSET_SPAN * wins
    vmem = pltpu.VMEM
    dma = pltpu.SemaphoreType.DMA
    out = pl.pallas_call(
        functools.partial(kernel, n_chan, n_tm),
        out_shape=pltpu.VMEM((pairs, chans, length), BF16),
        in_specs=[pl.BlockSpec(memory_space=pltpu.HBM)] * 5,
        out_specs=pl.BlockSpec(memory_space=pl.ANY),
        scratch_shapes=[
            vmem((wins, chans), jnp.int32),
            pltpu.SMEM((pairs,), jnp.int32),
            vmem((rows, length), BF16),
            vmem((edge, length), BF16),
            vmem((wins, chans), jnp.int32),
            vmem((length, length), BF16),
            vmem((2, length, length), BF16),
            vmem((2 * bins // 128, rows, 128), F32),
            vmem((2 * chans, wins), F32),
            vmem((wins, 2 * bins // 128, chans + OFFSET_SPAN, 128), F32),
            vmem((2, n_tm, length // 128, part, 128), BF16),
            vmem((2, n_tm, length // 128, part, 128), BF16),
            vmem((n_tm * part, length), F32),
            vmem((2, n_tm, part // 8, 8, length), BF16),
            dma((5,)),
            dma((OFFSET_SPAN // 8 + 1,)),
            dma((OFFSET_SPAN // 8 + 1,)),
            dma((2, n_tm)),
            dma((2, n_tm)),
            dma((2, n_tm)),
            dma((2, n_tm)),
            dma((2,)),
        ],
        compiler_params=pltpu.CompilerParams(
            collective_id=0, has_side_effects=True
        ),
        name="stacks",
    )(
        samples.reshape(rows, length),
        valid.T,
        offsets,
        jnp.asarray(forward_table(length)),
        jnp.asarray(inverse_table(length)),
    )
    return out[None]


def solution(mesh):
    body = functools.partial(per_device, mesh.shape["chan"], mesh.shape["tm"])
    return jax.shard_map(
        body,
        mesh=mesh,
        in_specs=(P("chan", "tm", None), P("chan", "tm"), P()),
        out_specs=P("tm", None, "chan", None),
        check_vma=False,
    )
```
